32 devices in a mesh: region: 4 (over z), row: 2 (over core), col: 4 (over y, x).
Axes of the slice: x: 2, y: 2, z: 4, core: 2. Of those that a mesh axis runs over, the one named last changes fastest.
Arguments:
- cam_jac: bfloat16 [3, 2, 256, 16384], P(None, None, None, 'region'), may hold values from -1 to 1
- point_rows: bfloat16 [3, 2, 4, 16384], P(None, None, None, 'region'), may hold values from -6 to 6
- track_images: int32 [3, 16384], P(None, 'region'), may hold values from 0 to 3, as said below
- track_counts: int32 [4], replicated, may hold values from 1 to 4096, 8192 in all
Outputs:
- factor: float32 [1024, 1024], P(('region', 'row'), 'col')
- solved: float32 [1024], replicated
The draws below stay inside these ranges and needn't reach their ends.
Inputs may be any that keep to these rules, and one draw needn't show every extreme that they name: `track_images`: each track's 3 entries are different images of the slab. `track_counts`: entry r counts region r's live tracks, which fill its first slots; later slots hold data that no output reads. The counts sum to 8192, and one region has exactly 4096.
All inputs are finite; a program needn't handle non-finite values.
Results may differ from the reference program's by a relative error of at most 0.0036.
Values may be sent and summed in bfloat16 or wider, within the bound.
A program may use at most 128 MiB of HBM per device.

```python
import math
import jax
import jax.numpy as jnp
import numpy as np
from jax import lax

PARAMS = 256
SLAB_IMAGES = 4
VIEWS = 3
BLOCK = 256
MEAN_TRACKS = 2048
SLOTS = 4096
REGIONS = 4
TRACKS = 16384
SLAB = 1024


def draw_track_images(key, part):
    first = jax.random.randint(key, (TRACKS,), 0, SLAB_IMAGES)
    offsets = jnp.arange(VIEWS, dtype=jnp.int32)[:, None]
    return ((first[None, :] + offsets) % SLAB_IMAGES).astype(jnp.int32)


def draw_cam_jac(key, part):
    subkeys = jax.random.split(key, 3)
    common = jnp.clip(jax.random.normal(subkeys[0], (1, 2, 1, TRACKS), jnp.float32), -4.0, 4.0)
    shared = jnp.clip(jax.random.normal(subkeys[1], (1, 2, PARAMS, TRACKS), jnp.float32), -4.0, 4.0)
    single = jnp.clip(jax.random.normal(subkeys[2], (VIEWS, 2, PARAMS, TRACKS), jnp.float32), -4.0, 4.0)
    entries = 0.7 * common + 2.0 * shared + single
    normalizer = 1.0 / jnp.sqrt(jnp.float32(5.0 * MEAN_TRACKS * REGIONS))
    return (entries * normalizer).astype(jnp.bfloat16)


def draw_point_rows(key, part):
    subkeys = jax.random.split(key, 3)
    ground = jax.random.normal(subkeys[0], (1, 2, 3, TRACKS), jnp.float32)
    single = jax.random.normal(subkeys[1], (VIEWS, 2, 3, TRACKS), jnp.float32)
    errors = jax.random.normal(subkeys[2], (VIEWS, 2, 1, TRACKS), jnp.float32)
    coords = ground + 0.3 * single
    joined = jnp.concatenate([coords, errors], axis=2)
    return jnp.clip(joined, -6.0, 6.0).astype(jnp.bfloat16)


def split_up(number_of, total, limit, lean):
    portions = [(1 << 20) // math.isqrt(grade ** lean) + 1 for grade in range(2, number_of + 1)]
    rest, given = total - limit - (number_of - 1), [1] * (number_of - 1)
    while rest > 0:
        movable = [i for i in range(number_of - 1) if given[i] < limit]
        pool, left = sum([portions[i] for i in movable]), rest
        for i in movable:
            extra = min(limit - given[i], max(1, left * portions[i] // pool), rest)
            given[i] = given[i] + extra
            rest = rest - extra
    return np.array([limit] + given)


def uneven(rng, number_of, total, reach, lean):
    if number_of == 2:
        one = jax.random.randint(rng, (), max(1, total - reach), min(reach, total - 1) + 1)
        return jnp.stack([one, total - one])
    tallies = jnp.asarray(split_up(number_of, total, reach, lean), jnp.int32)
    couples = (number_of - 1) // 2
    source_of, sink = tallies[1:1 + 2 * couples:2], tallies[2:2 + 2 * couples:2]
    room = jnp.minimum(source_of - 1, reach - sink)
    shifted = jax.random.randint(jax.random.fold_in(rng, 1), (couples,), 0, 1 << 20) % (room + 1)
    tallies = tallies.at[1:1 + 2 * couples:2].set(source_of - shifted).at[2:2 + 2 * couples:2].set(sink + shifted)
    return tallies[jax.random.permutation(jax.random.fold_in(rng, 2), number_of)]


def setup_inputs(seed: int = 0) -> dict:
    arg_keys = jax.random.split(jax.random.key(seed), 5)
    return {
        "cam_jac": draw_cam_jac(jax.random.fold_in(arg_keys[4], 71), 0),
        "point_rows": draw_point_rows(jax.random.fold_in(arg_keys[4], 71), 0),
        "track_images": draw_track_images(jax.random.fold_in(arg_keys[4], 71), 0),
        "track_counts": uneven(arg_keys[3], REGIONS, MEAN_TRACKS * REGIONS, SLOTS, 2).astype(jnp.int32),
    }


damping = 0.1
point_damping = 0.5

def lower_solve(factor_parts, first, second, third):
    diag_one, below_one, diag_two, below_far, below_two, diag_three = factor_parts
    out_one = first / diag_one
    out_two = (second - below_one * out_one) / diag_two
    out_three = (third - below_far * out_one - below_two * out_two) / diag_three
    return (out_one, out_two, out_three)

def block_terms(cam, points, selector):
    jac_point = points[:, :, 0:3].astype(jnp.float32)
    errors = points[:, :, 3].astype(jnp.float32)

    def entry(left, right):
        return lax.optimization_barrier(jnp.sum(jac_point[:, :, left] * jac_point[:, :, right], axis=(0, 1)))
    diag_one = jnp.sqrt(entry(0, 0) + point_damping)
    below_one = entry(1, 0) / diag_one
    below_far = entry(2, 0) / diag_one
    diag_two = jnp.sqrt(entry(1, 1) + point_damping - below_one * below_one)
    below_two = (entry(2, 1) - below_far * below_one) / diag_two
    diag_three = jnp.sqrt(entry(2, 2) + point_damping - below_far * below_far - below_two * below_two)
    factor_parts = (diag_one, below_one, diag_two, below_far, below_two, diag_three)
    coef = jnp.stack(lower_solve(factor_parts, jac_point[:, :, 0], jac_point[:, :, 1], jac_point[:, :, 2]), axis=0).astype(jnp.bfloat16)
    grads = [lax.optimization_barrier(jnp.sum(jac_point[:, :, comp] * errors, axis=(0, 1))) for comp in range(3)]
    point_step = jnp.stack(lower_solve(factor_parts, grads[0], grads[1], grads[2]), axis=0).astype(jnp.bfloat16)
    coef_wide = coef.astype(jnp.float32)
    products = cam[:, 0, :, None, :].astype(jnp.float32) * coef_wide[:, :, 0, :].transpose(1, 0, 2)[:, None, :, :]
    products = products + cam[:, 1, :, None, :].astype(jnp.float32) * coef_wide[:, :, 1, :].transpose(1, 0, 2)[:, None, :, :]
    schur = selector[0][:, None, None, :] * products[0][None]
    for view in range(1, selector.shape[0]):
        schur = schur + selector[view][:, None, None, :] * products[view][None]
    schur = schur.astype(jnp.bfloat16)
    pick = selector.astype(jnp.bfloat16)
    diagonal = jnp.einsum('krpb,kab->aprb', cam.astype(jnp.float32), pick.astype(jnp.float32), preferred_element_type=jnp.float32).astype(jnp.bfloat16)
    err_pick = (errors[None, :, :, :] * selector.transpose(1, 0, 2)[:, :, None, :]).astype(jnp.bfloat16)
    direct = jnp.einsum('krpb,akrb->ap', cam.astype(jnp.float32), err_pick.astype(jnp.float32), preferred_element_type=jnp.float32)
    coupled = jnp.einsum('apmb,mb->ap', schur.astype(jnp.float32), point_step.astype(jnp.float32), precision=lax.Precision.HIGHEST)
    return (schur, diagonal, direct - coupled)

def panel_factor(column, first_row, end_row):
    chol_block = jnp.linalg.cholesky(column[first_row:end_row])
    parts = [jnp.zeros((first_row, column.shape[1]), column.dtype), chol_block]
    if end_row < column.shape[0]:
        parts.append(lax.linalg.triangular_solve(chol_block, column[end_row:], left_side=False, lower=True, transpose_a=True))
    return jnp.concatenate(parts, axis=0)

def reference(cam_jac, point_rows, track_images, track_counts):

    def region_step(region, carry):
        count = track_counts[region]

        def block_step(block, inner):
            matrix, gradient = inner
            start = (region.astype(jnp.int32) * SLOTS + block.astype(jnp.int32) * BLOCK).astype(jnp.int32)
            cam = lax.dynamic_slice_in_dim(cam_jac, start, BLOCK, 3)
            points = lax.dynamic_slice_in_dim(point_rows, start, BLOCK, 3)
            images = lax.dynamic_slice_in_dim(track_images, start, BLOCK, 1)
            slot_ids = block.astype(jnp.int32) * BLOCK + jnp.arange(BLOCK, dtype=jnp.int32)
            live = (slot_ids < count).astype(jnp.float32)
            selector = (images[:, None, :] == jnp.arange(SLAB_IMAGES, dtype=jnp.int32)[None, :, None]).astype(jnp.float32) * live[None, None, :]
            schur, diagonal, grad = block_terms(cam, points, selector)
            flat = schur.reshape(SLAB, 3 * BLOCK)
            matrix = matrix - jnp.dot(flat.astype(jnp.float32), flat.T.astype(jnp.float32), preferred_element_type=jnp.float32)
            for image in range(SLAB_IMAGES):
                part = diagonal[image].reshape(PARAMS, 2 * BLOCK)
                update = jnp.dot(part.astype(jnp.float32), part.T.astype(jnp.float32), preferred_element_type=jnp.float32)
                matrix = matrix.at[image * PARAMS:(image + 1) * PARAMS, image * PARAMS:(image + 1) * PARAMS].add(update)
            gradient = gradient + grad.reshape(SLAB)
            return (matrix, gradient)
        blocks = ((count + BLOCK - 1) // BLOCK).astype(jnp.int32)
        return lax.fori_loop(jnp.int32(0), blocks, block_step, carry)
    start_state = (jnp.zeros((SLAB, SLAB), jnp.float32), jnp.zeros((SLAB,), jnp.float32))
    matrix, gradient = lax.fori_loop(0, REGIONS, region_step, start_state)
    matrix = matrix + damping * jnp.eye(SLAB, dtype=jnp.float32)
    columns = []
    pieces = []
    for panel in range(SLAB_IMAGES):
        first_row = panel * PARAMS
        end_row = first_row + PARAMS
        factored = panel_factor(matrix[:, first_row:end_row], first_row, end_row)
        columns.append(factored)
        part_z = lax.linalg.triangular_solve(factored[first_row:end_row], gradient[first_row:end_row][:, None], left_side=True, lower=True)[:, 0]
        pieces.append(part_z)
        below = jnp.concatenate([jnp.zeros((end_row, PARAMS), factored.dtype), factored[end_row:]], axis=0)
        gradient = gradient - jnp.dot(below, part_z, precision=lax.Precision.HIGHEST)
        matrix = matrix - jnp.dot(factored, factored.T, precision=lax.Precision.HIGHEST)
    return (jnp.concatenate(columns, axis=1), jnp.concatenate(pieces))
```

```python
import functools

import jax
import jax.numpy as jnp
from jax import lax
from jax.experimental import pallas as pl
from jax.experimental.pallas import tpu as pltpu
from jax.sharding import PartitionSpec as P

SLAB_IMAGES = 4
BLOCK = 512
TILE = 128
EXTRA = 8
VMEM_LIMIT = 60 * 1024 * 1024

damping = 0.1
point_damping = 0.5

NT = (((1,), (1,)), ((), ()))


def point_terms(pts):
    views = len(pts)
    pairs = [(k, r) for k in range(views) for r in range(2)]

    def entry(left, right):
        return sum(pts[k][r][left] * pts[k][r][right] for k, r in pairs)

    d1 = jnp.sqrt(entry(0, 0) + point_damping)
    b1 = entry(1, 0) / d1
    bf = entry(2, 0) / d1
    d2 = jnp.sqrt(entry(1, 1) + point_damping - b1 * b1)
    b2 = (entry(2, 1) - bf * b1) / d2
    d3 = jnp.sqrt(entry(2, 2) + point_damping - bf * bf - b2 * b2)

    def solve(first, second, third):
        o1 = first / d1
        o2 = (second - b1 * o1) / d2
        o3 = (third - bf * o1 - b2 * o2) / d3
        return [o.astype(jnp.bfloat16).astype(jnp.float32) for o in (o1, o2, o3)]

    coef = {(k, r): solve(*pts[k][r][0:3]) for k, r in pairs}
    step = solve(*[entry(c, 3) for c in range(3)])
    return coef, step


def accumulate_kernel(regions, pos_ref, cam_ref, pts_ref, img_ref, out_ref, acc, rows, cols, dr, dc):
    views = cam_ref.shape[0]
    params = cam_ref.shape[2]
    block = cam_ref.shape[3]
    half = params // 2
    tile_rows = SLAB_IMAGES * half
    step = pl.program_id(0)
    count = pos_ref[0]
    row_at = pos_ref[1]
    col_at = pos_ref[2]

    @pl.when(step == 0)
    def _():
        acc[...] = jnp.zeros_like(acc)
        rows[tile_rows:, :] = jnp.zeros_like(rows[tile_rows:, :])
        dr[half:, :] = jnp.zeros_like(dr[half:, :])

    @pl.when(step * block < count)
    def _():
        slot = step * block + lax.broadcasted_iota(jnp.int32, (1, block), 1)
        live = slot < count
        pts = []
        for k in range(views):
            pts.append([])
            for r in range(2):
                wide = pts_ref[k, r].astype(jnp.float32)
                pts[k].append([wide[c : c + 1, :] for c in range(4)])
        coef, y = point_terms(pts)
        images = [img_ref[k : k + 1, :] for k in range(views)]

        def picks(image):
            return [(images[k] == image) & live for k in range(views)]

        def pick(masks, values):
            out = jnp.zeros_like(values[0])
            for mask, value in zip(masks, values):
                out = jnp.where(mask, value, out)
            return out

        def chosen(image):
            masks = picks(image)
            c = [
                [pick(masks, [coef[k, r][m] for k in range(views)]) for r in range(2)]
                for m in range(3)
            ]
            return masks, c

        zero = jnp.zeros((15, block), jnp.float32)
        for m in range(3):
            rows[tile_rows : tile_rows + 16, m * block : (m + 1) * block] = jnp.concatenate(
                [y[m], zero], axis=0
            ).astype(jnp.bfloat16)

        sub = 16
        col_masks, col_c = chosen(col_at)
        for r in range(2):
            err = pick(col_masks, [pts[k][r][3] for k in range(views)])
            dr[half : half + 16, r * block : (r + 1) * block] = jnp.concatenate(
                [err, zero], axis=0
            ).astype(jnp.bfloat16)

        def widen(mask):
            return jnp.broadcast_to(mask.astype(jnp.int32), (sub, block)) != 0

        def products(jac, c):
            return [jac[0] * c[m][0] + jac[1] * c[m][1] for m in range(3)]

        def col_chunk(i, _):
            at = pl.multiple_of(i * sub, sub)
            jac = []
            for r in range(2):
                j = [cam_ref[k, r, pl.ds(at, sub), :].astype(jnp.float32) for k in range(views)]
                picked = pick([widen(m) for m in col_masks], j)
                dc[pl.ds(at, sub), r * block : (r + 1) * block] = picked.astype(jnp.bfloat16)
                jac.append(picked)
            for m, value in enumerate(products(jac, col_c)):
                cols[pl.ds(at, sub), m * block : (m + 1) * block] = value.astype(jnp.bfloat16)
            return 0

        lax.fori_loop(0, params // sub, col_chunk, 0)

        row_chosen = [chosen(a) for a in range(SLAB_IMAGES)]

        def row_chunk(i, _):
            at = pl.multiple_of(i * sub, sub)
            src = pl.multiple_of(row_at * half + i * sub, sub)
            j = [
                [cam_ref[k, r, pl.ds(src, sub), :].astype(jnp.float32) for k in range(views)]
                for r in range(2)
            ]
            for a in range(SLAB_IMAGES):
                masks, c = row_chosen[a]
                wide = [widen(m) for m in masks]
                jac = [
                    jnp.where(wide[0], j[r][0], jnp.where(wide[1], j[r][1], j[r][2]))
                    for r in range(2)
                ]
                for m, value in enumerate(products(jac, c)):
                    rows[pl.ds(a * half + at, sub), m * block : (m + 1) * block] = value.astype(
                        jnp.bfloat16
                    )
            return 0

        lax.fori_loop(0, half // sub, row_chunk, 0)
        dr[0:half, :] = dc[pl.ds(pl.multiple_of(row_at * half, half), half), :]
        acc[...] -= lax.dot_general(
            rows[...], cols[...], NT, preferred_element_type=jnp.float32
        )
        direct = lax.dot_general(dr[...], dc[...], NT, preferred_element_type=jnp.float32)
        at = pl.ds(pl.multiple_of(col_at * half, half), half)
        acc[at, :] += direct[0:half]
        acc[tile_rows : tile_rows + 16, :] += direct[half : half + 16]

    @pl.when(step == pl.num_programs(0) - 1)
    def _():
        chunk = tile_rows // regions
        for r in range(regions):
            out_ref[r, 0:chunk, :] = acc[r * chunk : (r + 1) * chunk, :]
            out_ref[r, chunk : chunk + EXTRA, :] = acc[tile_rows : tile_rows + EXTRA, :]


def accumulate(cam_jac, point_rows, track_images, pos, regions):
    views, _, params, slots = cam_jac.shape
    block = min(BLOCK, slots)
    half = params // 2
    tile_rows = SLAB_IMAGES * half
    chunk = tile_rows // regions

    def at(i, pos_ref):
        return jnp.minimum(i, (pos_ref[0] - 1) // block)

    return pl.pallas_call(
        functools.partial(accumulate_kernel, regions),
        out_shape=jax.ShapeDtypeStruct((regions, chunk + EXTRA, params), jnp.float32),
        grid_spec=pltpu.PrefetchScalarGridSpec(
            num_scalar_prefetch=1,
            grid=(slots // block,),
            in_specs=[
                pl.BlockSpec((views, 2, params, block), lambda i, p: (0, 0, 0, at(i, p))),
                pl.BlockSpec((views, 2, 4, block), lambda i, p: (0, 0, 0, at(i, p))),
                pl.BlockSpec((views, block), lambda i, p: (0, at(i, p))),
            ],
            out_specs=pl.BlockSpec((regions, chunk + EXTRA, params), lambda i, p: (0, 0, 0)),
            scratch_shapes=[
                pltpu.VMEM((tile_rows + 16, params), jnp.float32),
                pltpu.VMEM((tile_rows + 16, 3 * block), jnp.bfloat16),
                pltpu.VMEM((params, 3 * block), jnp.bfloat16),
                pltpu.VMEM((half + 16, 2 * block), jnp.bfloat16),
                pltpu.VMEM((params, 2 * block), jnp.bfloat16),
            ],
        ),
        compiler_params=pltpu.CompilerParams(
            dimension_semantics=("arbitrary",), vmem_limit_bytes=VMEM_LIMIT
        ),
        name="accumulate",
    )(pos, cam_jac, point_rows, track_images)


def eliminate(tile):
    groups = TILE // 8
    sub = lax.broadcasted_iota(jnp.int32, (8, TILE), 0)
    lane = lax.broadcasted_iota(jnp.int32, (8, TILE), 1)
    d = [tile[8 * g : 8 * g + 8, :] for g in range(groups)]
    e = [(lane == sub + 8 * g).astype(jnp.float32) for g in range(groups)]
    for j in range(TILE):
        g, s = j // 8, j % 8
        row = d[g][s : s + 1, :]
        row_e = e[g][s : s + 1, :]
        pivot = jnp.broadcast_to(row[:, j : j + 1], (1, TILE))
        inv = 1.0 / pivot
        srow = jnp.broadcast_to(row * inv, (8, TILE))
        srow_e = jnp.broadcast_to(row_e * inv, (8, TILE))
        root = lax.rsqrt(pivot)
        for i in range(g, groups):
            col = jnp.broadcast_to(d[i][:, j : j + 1], (8, TILE))
            if i == g:
                col = jnp.where(sub > s, col, 0.0)
            new_d = d[i] - col * srow
            new_e = e[i] - col * srow_e
            if i == g:
                new_d = jnp.where(sub == s, d[i] * root, new_d)
                new_e = jnp.where(sub == s, e[i] * root, new_e)
            d[i] = new_d
            e[i] = new_e
    u = jnp.concatenate([jnp.where(lane >= sub + 8 * g, d[g], 0.0) for g in range(groups)], axis=0)
    return u, jnp.concatenate(e, axis=0)


def factor_kernel(regions, params, pos_ref, all_ref, factor_ref, solved_ref, a_ref, linv_ref):
    total = SLAB_IMAGES * params
    half = params // 2
    chunk = SLAB_IMAGES * half // regions
    for r in range(regions):
        for c in range(2):
            first = (r * chunk) // half * params + c * half + (r * chunk) % half
            for j in range(SLAB_IMAGES):
                a_ref[first : first + chunk, j * params : (j + 1) * params] = all_ref[
                    (r * 2 + c) * SLAB_IMAGES + j, 0:chunk, :
                ]
    for j in range(SLAB_IMAGES):
        a_ref[total : total + EXTRA, j * params : (j + 1) * params] = all_ref[
            j, chunk : chunk + EXTRA, :
        ]
    panels = total // TILE
    eye_r = lax.broadcasted_iota(jnp.int32, (TILE, TILE), 0)
    eye_c = lax.broadcasted_iota(jnp.int32, (TILE, TILE), 1)
    damp = jnp.where(eye_r == eye_c, damping, 0.0).astype(jnp.float32)

    def panel(n, _):
        at = pl.ds(pl.multiple_of(n * TILE, TILE), TILE)
        upper, linv = eliminate(a_ref[at, at] + damp)
        a_ref[at, at] = upper.T
        linv_ref[...] = linv
        for s in range(panels):

            @pl.when(n == s)
            def _():
                lo = s * TILE
                hi = lo + TILE
                below = lax.dot_general(
                    a_ref[hi : total + EXTRA, lo:hi],
                    linv_ref[...],
                    NT,
                    precision=lax.Precision.HIGHEST,
                    preferred_element_type=jnp.float32,
                )
                a_ref[hi : total + EXTRA, lo:hi] = below
                col = hi
                while col < total:
                    width = 2 * TILE if col % (2 * TILE) == 0 else TILE
                    a_ref[col : total + EXTRA, col : col + width] -= lax.dot_general(
                        a_ref[col : total + EXTRA, lo:hi],
                        a_ref[col : col + width, lo:hi],
                        NT,
                        precision=lax.Precision.HIGHEST,
                        preferred_element_type=jnp.float32,
                    )
                    col += width

        return 0

    lax.fori_loop(0, panels, panel, 0)
    row_block = factor_ref.shape[0]
    first_row = pl.multiple_of(pos_ref[3] * row_block, row_block)
    first_col = pl.multiple_of(pos_ref[2] * params, params)
    held = a_ref[pl.ds(first_row, row_block), pl.ds(first_col, params)]
    at_row = first_row + lax.broadcasted_iota(jnp.int32, held.shape, 0)
    at_col = first_col + lax.broadcasted_iota(jnp.int32, held.shape, 1)
    factor_ref[...] = jnp.where(at_row >= at_col, held, 0.0)
    solved_ref[...] = a_ref[total : total + EXTRA, :]


def factorize(everything, pos, regions, params, row_block):
    total = SLAB_IMAGES * params
    return pl.pallas_call(
        functools.partial(factor_kernel, regions, params),
        out_shape=(
            jax.ShapeDtypeStruct((row_block, params), jnp.float32),
            jax.ShapeDtypeStruct((EXTRA, total), jnp.float32),
        ),
        in_specs=[
            pl.BlockSpec(memory_space=pltpu.SMEM),
            pl.BlockSpec(memory_space=pltpu.VMEM),
        ],
        out_specs=(
            pl.BlockSpec(memory_space=pltpu.VMEM),
            pl.BlockSpec(memory_space=pltpu.VMEM),
        ),
        scratch_shapes=[
            pltpu.VMEM((total + EXTRA, total), jnp.float32),
            pltpu.VMEM((TILE, TILE), jnp.float32),
        ],
        compiler_params=pltpu.CompilerParams(vmem_limit_bytes=VMEM_LIMIT),
        name="factorize",
    )(pos, everything)


def on_device(cam_jac, point_rows, track_images, track_counts):
    regions = lax.axis_size("region")
    row_count = lax.axis_size("row")
    region_at = lax.axis_index("region")
    row_at = lax.axis_index("row")
    col_at = lax.axis_index("col")
    params = cam_jac.shape[2]
    row_block = SLAB_IMAGES * params // (regions * row_count)
    pos = jnp.stack(
        [track_counts[region_at], row_at, col_at, region_at * row_count + row_at]
    ).astype(jnp.int32)
    tile = accumulate(cam_jac, point_rows, track_images, pos, regions)
    summed = lax.psum_scatter(tile, "region", scatter_dimension=0, tiled=False)
    everything = lax.all_gather(summed, ("region", "row", "col"), axis=0, tiled=False)
    factor, solved = factorize(everything, pos, regions, params, row_block)
    return (factor, solved[0])


def solution(mesh):
    in_specs = (
        P(None, None, None, "region"),
        P(None, None, None, "region"),
        P(None, "region"),
        P(),
    )
    out_specs = (P(("region", "row"), "col"), P())
    return jax.shard_map(
        on_device, mesh=mesh, in_specs=in_specs, out_specs=out_specs, check_vma=False
    )
```

```python
import functools

import jax
import jax.numpy as jnp
from jax import lax
from jax.experimental import pallas as pl
from jax.experimental.pallas import tpu as pltpu
from jax.sharding import PartitionSpec as P

SLAB_IMAGES = 4
BLOCK = 512
TILE = 128
EXTRA = 8
PIVOTS = 8
VMEM_LIMIT = 60 * 1024 * 1024

damping = 0.1
point_damping = 0.5

NT = (((1,), (1,)), ((), ()))


def point_terms(pts):
    views = len(pts)
    pairs = [(k, r) for k in range(views) for r in range(2)]

    def entry(left, right):
        return sum(pts[k][r][left] * pts[k][r][right] for k, r in pairs)

    d1 = jnp.sqrt(entry(0, 0) + point_damping)
    b1 = entry(1, 0) / d1
    bf = entry(2, 0) / d1
    d2 = jnp.sqrt(entry(1, 1) + point_damping - b1 * b1)
    b2 = (entry(2, 1) - bf * b1) / d2
    d3 = jnp.sqrt(entry(2, 2) + point_damping - bf * bf - b2 * b2)

    def solve(first, second, third):
        o1 = first / d1
        o2 = (second - b1 * o1) / d2
        o3 = (third - bf * o1 - b2 * o2) / d3
        return [o.astype(jnp.bfloat16).astype(jnp.float32) for o in (o1, o2, o3)]

    coef = {(k, r): solve(*pts[k][r][0:3]) for k, r in pairs}
    step = solve(*[entry(c, 3) for c in range(3)])
    return coef, step


def accumulate_kernel(regions, pos_ref, cam_ref, pts_ref, img_ref, out_ref, acc, rows, cols, dr, dc):
    views = cam_ref.shape[0]
    params = cam_ref.shape[2]
    block = cam_ref.shape[3]
    half = params // 2
    tile_rows = SLAB_IMAGES * half
    step = pl.program_id(0)
    count = pos_ref[0]
    row_at = pos_ref[1]
    col_at = pos_ref[2]

    @pl.when(step == 0)
    def _():
        acc[...] = jnp.zeros_like(acc)
        rows[tile_rows:, :] = jnp.zeros_like(rows[tile_rows:, :])
        dr[half:, :] = jnp.zeros_like(dr[half:, :])

    @pl.when(step * block < count)
    def _():
        slot = step * block + lax.broadcasted_iota(jnp.int32, (1, block), 1)
        live = slot < count
        pts = []
        for k in range(views):
            pts.append([])
            for r in range(2):
                wide = pts_ref[k, r].astype(jnp.float32)
                pts[k].append([wide[c : c + 1, :] for c in range(4)])
        coef, y = point_terms(pts)
        images = [img_ref[k : k + 1, :] for k in range(views)]

        def picks(image):
            return [(images[k] == image) & live for k in range(views)]

        def pick(masks, values):
            out = jnp.zeros_like(values[0])
            for mask, value in zip(masks, values):
                out = jnp.where(mask, value, out)
            return out

        def chosen(image):
            masks = picks(image)
            c = [
                [pick(masks, [coef[k, r][m] for k in range(views)]) for r in range(2)]
                for m in range(3)
            ]
            return masks, c

        zero = jnp.zeros((15, block), jnp.float32)
        for m in range(3):
            rows[tile_rows : tile_rows + 16, m * block : (m + 1) * block] = jnp.concatenate(
                [y[m], zero], axis=0
            ).astype(jnp.bfloat16)

        sub = 16
        col_masks, col_c = chosen(col_at)
        for r in range(2):
            err = pick(col_masks, [pts[k][r][3] for k in range(views)])
            dr[half : half + 16, r * block : (r + 1) * block] = jnp.concatenate(
                [err, zero], axis=0
            ).astype(jnp.bfloat16)

        def widen(mask):
            return jnp.broadcast_to(mask.astype(jnp.int32), (sub, block)) != 0

        def products(jac, c):
            return [jac[0] * c[m][0] + jac[1] * c[m][1] for m in range(3)]

        def col_chunk(i, _):
            at = pl.multiple_of(i * sub, sub)
            jac = []
            for r in range(2):
                j = [cam_ref[k, r, pl.ds(at, sub), :].astype(jnp.float32) for k in range(views)]
                picked = pick([widen(m) for m in col_masks], j)
                dc[pl.ds(at, sub), r * block : (r + 1) * block] = picked.astype(jnp.bfloat16)
                jac.append(picked)
            for m, value in enumerate(products(jac, col_c)):
                cols[pl.ds(at, sub), m * block : (m + 1) * block] = value.astype(jnp.bfloat16)
            return 0

        lax.fori_loop(0, params // sub, col_chunk, 0)

        row_chosen = [chosen(a) for a in range(SLAB_IMAGES)]

        def row_chunk(i, _):
            at = pl.multiple_of(i * sub, sub)
            src = pl.multiple_of(row_at * half + i * sub, sub)
            j = [
                [cam_ref[k, r, pl.ds(src, sub), :].astype(jnp.float32) for k in range(views)]
                for r in range(2)
            ]
            for a in range(SLAB_IMAGES):
                masks, c = row_chosen[a]
                wide = [widen(m) for m in masks]
                jac = [
                    jnp.where(wide[0], j[r][0], jnp.where(wide[1], j[r][1], j[r][2]))
                    for r in range(2)
                ]
                for m, value in enumerate(products(jac, c)):
                    rows[pl.ds(a * half + at, sub), m * block : (m + 1) * block] = value.astype(
                        jnp.bfloat16
                    )
            return 0

        lax.fori_loop(0, half // sub, row_chunk, 0)
        dr[0:half, :] = dc[pl.ds(pl.multiple_of(row_at * half, half), half), :]
        acc[...] -= lax.dot_general(
            rows[...], cols[...], NT, preferred_element_type=jnp.float32
        )
        direct = lax.dot_general(dr[...], dc[...], NT, preferred_element_type=jnp.float32)
        at = pl.ds(pl.multiple_of(col_at * half, half), half)
        acc[at, :] += direct[0:half]
        acc[tile_rows : tile_rows + 16, :] += direct[half : half + 16]

    @pl.when(step == pl.num_programs(0) - 1)
    def _():
        chunk = tile_rows // regions
        for r in range(regions):
            out_ref[r, 0:chunk, :] = acc[r * chunk : (r + 1) * chunk, :]
            out_ref[r, chunk : chunk + EXTRA, :] = acc[tile_rows : tile_rows + EXTRA, :]


def accumulate(cam_jac, point_rows, track_images, pos, regions):
    views, _, params, slots = cam_jac.shape
    block = min(BLOCK, slots)
    half = params // 2
    tile_rows = SLAB_IMAGES * half
    chunk = tile_rows // regions

    def at(i, pos_ref):
        return jnp.minimum(i, (pos_ref[0] - 1) // block)

    return pl.pallas_call(
        functools.partial(accumulate_kernel, regions),
        out_shape=jax.ShapeDtypeStruct((regions, chunk + EXTRA, params), jnp.float32),
        grid_spec=pltpu.PrefetchScalarGridSpec(
            num_scalar_prefetch=1,
            grid=(slots // block,),
            in_specs=[
                pl.BlockSpec((views, 2, params, block), lambda i, p: (0, 0, 0, at(i, p))),
                pl.BlockSpec((views, 2, 4, block), lambda i, p: (0, 0, 0, at(i, p))),
                pl.BlockSpec((views, block), lambda i, p: (0, at(i, p))),
            ],
            out_specs=pl.BlockSpec((regions, chunk + EXTRA, params), lambda i, p: (0, 0, 0)),
            scratch_shapes=[
                pltpu.VMEM((tile_rows + 16, params), jnp.float32),
                pltpu.VMEM((tile_rows + 16, 3 * block), jnp.bfloat16),
                pltpu.VMEM((params, 3 * block), jnp.bfloat16),
                pltpu.VMEM((half + 16, 2 * block), jnp.bfloat16),
                pltpu.VMEM((params, 2 * block), jnp.bfloat16),
            ],
        ),
        compiler_params=pltpu.CompilerParams(
            dimension_semantics=("arbitrary",), vmem_limit_bytes=VMEM_LIMIT
        ),
        name="accumulate",
    )(pos, cam_jac, point_rows, track_images)


def eliminate(tile):
    groups = TILE // 8
    sub = lax.broadcasted_iota(jnp.int32, (8, TILE), 0)
    lane = lax.broadcasted_iota(jnp.int32, (8, TILE), 1)
    d = [tile[8 * g : 8 * g + 8, :] for g in range(groups)]
    e = [(lane == sub + 8 * g).astype(jnp.float32) for g in range(groups)]
    for j in range(0, TILE, PIVOTS):
        g, s = j // 8, j % 8
        ids = range(PIVOTS)
        rd = [d[g][s + q : s + q + 1, :] for q in ids]
        re = [e[g][s + q : s + q + 1, :] for q in ids]
        block = {
            (p, q): jnp.broadcast_to(rd[p][:, j + q : j + q + 1], (1, TILE))
            for p in ids
            for q in ids
            if q >= p
        }
        low, inv = {}, []
        for p in ids:
            inv.append(1.0 / block[p, p])
            for q in range(p + 1, PIVOTS):
                low[q, p] = block[p, q] * inv[p]
            for q in range(p + 1, PIVOTS):
                for r in range(q, PIVOTS):
                    block[q, r] = block[q, r] - low[q, p] * block[p, r]
                rd[q] = rd[q] - low[q, p] * rd[p]
                re[q] = re[q] - low[q, p] * re[p]
        roots = [lax.rsqrt(block[p, p]) for p in ids]
        wd = [rd[p] * inv[p] for p in ids]
        we = [re[p] * inv[p] for p in ids]
        for q in reversed(ids):
            for p in range(q):
                wd[p] = wd[p] - low[q, p] * wd[q]
                we[p] = we[p] - low[q, p] * we[q]
        wd = [jnp.broadcast_to(w, (8, TILE)) for w in wd]
        we = [jnp.broadcast_to(w, (8, TILE)) for w in we]
        for i in range(g, groups):
            if i == g and s + PIVOTS == 8:
                new_d, new_e = d[i], e[i]
            else:
                new_d, new_e = d[i], e[i]
                for p in ids:
                    col = jnp.broadcast_to(d[i][:, j + p : j + p + 1], (8, TILE))
                    if i == g:
                        col = jnp.where(sub >= s + PIVOTS, col, 0.0)
                    new_d = new_d - col * wd[p]
                    new_e = new_e - col * we[p]
            if i == g:
                for p in ids:
                    new_d = jnp.where(sub == s + p, rd[p] * roots[p], new_d)
                    new_e = jnp.where(sub == s + p, re[p] * roots[p], new_e)
            d[i], e[i] = new_d, new_e
    u = jnp.concatenate([jnp.where(lane >= sub + 8 * g, d[g], 0.0) for g in range(groups)], axis=0)
    return u, jnp.concatenate(e, axis=0)


def factor_kernel(regions, params, pos_ref, all_ref, factor_ref, solved_ref, a_ref, linv_ref):
    total = SLAB_IMAGES * params
    half = params // 2
    chunk = SLAB_IMAGES * half // regions
    for r in range(regions):
        for c in range(2):
            first = (r * chunk) // half * params + c * half + (r * chunk) % half
            for j in range((r * chunk) // half + 1):
                a_ref[first : first + chunk, j * params : (j + 1) * params] = all_ref[
                    (r * 2 + c) * SLAB_IMAGES + j, 0:chunk, :
                ]
    for j in range(SLAB_IMAGES):
        a_ref[total : total + EXTRA, j * params : (j + 1) * params] = all_ref[
            j * half // chunk * 2 * SLAB_IMAGES + j, chunk : chunk + EXTRA, :
        ]
    panels = total // TILE
    eye_r = lax.broadcasted_iota(jnp.int32, (TILE, TILE), 0)
    eye_c = lax.broadcasted_iota(jnp.int32, (TILE, TILE), 1)
    damp = jnp.where(eye_r == eye_c, damping, 0.0).astype(jnp.float32)

    def panel(n, _):
        at = pl.ds(pl.multiple_of(n * TILE, TILE), TILE)
        upper, linv = eliminate(a_ref[at, at] + damp)
        a_ref[at, at] = upper.T
        linv_ref[...] = linv
        for s in range(panels):

            @pl.when(n == s)
            def _():
                lo = s * TILE
                hi = lo + TILE
                below = lax.dot_general(
                    a_ref[hi : total + EXTRA, lo:hi],
                    linv_ref[...],
                    NT,
                    precision=lax.Precision.HIGHEST,
                    preferred_element_type=jnp.float32,
                )
                a_ref[hi : total + EXTRA, lo:hi] = below
                col = hi
                while col < total:
                    width = 2 * TILE if col % (2 * TILE) == 0 else TILE
                    a_ref[col : total + EXTRA, col : col + width] -= lax.dot_general(
                        a_ref[col : total + EXTRA, lo:hi],
                        a_ref[col : col + width, lo:hi],
                        NT,
                        precision=lax.Precision.HIGHEST,
                        preferred_element_type=jnp.float32,
                    )
                    col += width

        return 0

    lax.fori_loop(0, panels, panel, 0)
    row_block = factor_ref.shape[0]
    first_row = pl.multiple_of(pos_ref[3] * row_block, row_block)
    first_col = pl.multiple_of(pos_ref[2] * params, params)
    held = a_ref[pl.ds(first_row, row_block), pl.ds(first_col, params)]
    at_row = first_row + lax.broadcasted_iota(jnp.int32, held.shape, 0)
    at_col = first_col + lax.broadcasted_iota(jnp.int32, held.shape, 1)
    factor_ref[...] = jnp.where(at_row >= at_col, held, 0.0)
    solved_ref[...] = a_ref[total : total + EXTRA, :]


def factorize(everything, pos, regions, params, row_block):
    total = SLAB_IMAGES * params
    return pl.pallas_call(
        functools.partial(factor_kernel, regions, params),
        out_shape=(
            jax.ShapeDtypeStruct((row_block, params), jnp.float32),
            jax.ShapeDtypeStruct((EXTRA, total), jnp.float32),
        ),
        in_specs=[
            pl.BlockSpec(memory_space=pltpu.SMEM),
            pl.BlockSpec(memory_space=pltpu.VMEM),
        ],
        out_specs=(
            pl.BlockSpec(memory_space=pltpu.VMEM),
            pl.BlockSpec(memory_space=pltpu.VMEM),
        ),
        scratch_shapes=[
            pltpu.VMEM((total + EXTRA, total), jnp.float32),
            pltpu.VMEM((TILE, TILE), jnp.float32),
        ],
        compiler_params=pltpu.CompilerParams(vmem_limit_bytes=VMEM_LIMIT),
        name="factorize",
    )(pos, everything)


def exchange_kernel(regions, tile_ref, all_ref, recv, mine, sum_send, sum_recv, sends, arrived):
    half = recv.shape[2] // 2
    chunk = SLAB_IMAGES * half // regions
    region_at = lax.axis_index("region")
    row_at = lax.axis_index("row")
    col_at = lax.axis_index("col")

    def device(region, row, col):
        return {"region": region, "row": row, "col": col}

    def plus(at, by, size):
        return lax.rem(at + by, size)

    def needed(region, col):
        return (region * chunk) // half >= col

    def index(region, row, col):
        return (region * 2 + row) * SLAB_IMAGES + col

    partner = device(region_at, 1 - row_at, col_at)
    along = [device(plus(region_at, d, regions), row_at, col_at) for d in range(1, regions)]
    across = [device(region_at, row_at, plus(col_at, d, SLAB_IMAGES)) for d in range(1, SLAB_IMAGES)]
    barrier = pltpu.get_barrier_semaphore()
    for peer in [partner] + along + across:
        pl.semaphore_signal(barrier, inc=1, device_id=peer, device_id_type=pl.DeviceIdType.MESH)
    pl.semaphore_wait(barrier, regions + SLAB_IMAGES - 1)

    def part(d):
        to = plus(region_at, d, regions)
        return to, pltpu.make_async_remote_copy(
            src_ref=tile_ref.at[to],
            dst_ref=recv.at[d - 1],
            send_sem=sum_send.at[d - 1],
            recv_sem=sum_recv.at[d - 1],
            device_id=device(to, row_at, col_at),
            device_id_type=pl.DeviceIdType.MESH,
        )

    for d in range(1, regions):
        to, copy = part(d)

        @pl.when(needed(to, col_at))
        def _():
            copy.start()

    me = index(region_at, row_at, col_at)

    @pl.when(needed(region_at, col_at))
    def _():
        for d in range(1, regions):
            part(d)[1].wait_recv()
        total = tile_ref[region_at]
        for d in range(1, regions):
            total = total + recv[d - 1]
        mine[...] = total
        all_ref[me] = total

    for d in range(1, regions):
        to, copy = part(d)

        @pl.when(needed(to, col_at))
        def _():
            copy.wait_send()

    started = []

    def send(when, src, block, peer):
        copy = pltpu.make_async_remote_copy(
            src_ref=src,
            dst_ref=all_ref.at[block],
            send_sem=sends.at[len(started)],
            recv_sem=arrived.at[block],
            device_id=peer,
            device_id_type=pl.DeviceIdType.MESH,
        )
        started.append((when, copy))

        @pl.when(when)
        def _():
            copy.start()

    def arrive(when, block):
        copy = pltpu.make_async_remote_copy(
            src_ref=all_ref.at[block],
            dst_ref=all_ref.at[block],
            send_sem=sends.at[0],
            recv_sem=arrived.at[block],
            device_id=partner,
            device_id_type=pl.DeviceIdType.MESH,
        )

        @pl.when(when)
        def _():
            copy.wait_recv()

    ok = needed(region_at, col_at)
    for peer in along + across + [partner]:
        send(ok, mine, me, peer)
    for d in range(1, regions):
        origin = plus(region_at, d, regions)
        block = index(origin, row_at, col_at)
        ok = needed(origin, col_at)
        arrive(ok, block)
        for peer in across + [partner]:
            send(ok, all_ref.at[block], block, peer)
    for rd in range(regions):
        for cd in range(1, SLAB_IMAGES):
            origin = plus(region_at, rd, regions)
            col = plus(col_at, cd, SLAB_IMAGES)
            block = index(origin, row_at, col)
            ok = needed(origin, col)
            arrive(ok, block)
            send(ok, all_ref.at[block], block, partner)
    for rd in range(regions):
        for cd in range(SLAB_IMAGES):
            origin = plus(region_at, rd, regions)
            col = plus(col_at, cd, SLAB_IMAGES)
            arrive(needed(origin, col), index(origin, 1 - row_at, col))
    for when, copy in started:

        @pl.when(when)
        def _():
            copy.wait_send()


def exchange(tile):
    regions, depth, params = tile.shape
    blocks = regions * 2 * SLAB_IMAGES
    return pl.pallas_call(
        functools.partial(exchange_kernel, regions),
        out_shape=jax.ShapeDtypeStruct((blocks, depth, params), jnp.float32),
        in_specs=[pl.BlockSpec(memory_space=pltpu.VMEM)],
        out_specs=pl.BlockSpec(memory_space=pltpu.VMEM),
        scratch_shapes=[
            pltpu.VMEM((regions - 1, depth, params), jnp.float32),
            pltpu.VMEM((depth, params), jnp.float32),
            pltpu.SemaphoreType.DMA((regions - 1,)),
            pltpu.SemaphoreType.DMA((regions - 1,)),
            pltpu.SemaphoreType.DMA((blocks,)),
            pltpu.SemaphoreType.DMA((blocks,)),
        ],
        compiler_params=pltpu.CompilerParams(
            collective_id=0, has_side_effects=True, vmem_limit_bytes=VMEM_LIMIT
        ),
        name="exchange",
    )(tile)


def on_device(cam_jac, point_rows, track_images, track_counts):
    regions = lax.axis_size("region")
    row_count = lax.axis_size("row")
    region_at = lax.axis_index("region")
    row_at = lax.axis_index("row")
    col_at = lax.axis_index("col")
    params = cam_jac.shape[2]
    row_block = SLAB_IMAGES * params // (regions * row_count)
    pos = jnp.stack(
        [track_counts[region_at], row_at, col_at, region_at * row_count + row_at]
    ).astype(jnp.int32)
    tile = accumulate(cam_jac, point_rows, track_images, pos, regions)
    everything = exchange(tile)
    factor, solved = factorize(everything, pos, regions, params, row_block)
    return (factor, solved[0])


def solution(mesh):
    in_specs = (
        P(None, None, None, "region"),
        P(None, None, None, "region"),
        P(None, "region"),
        P(),
    )
    out_specs = (P(("region", "row"), "col"), P())
    return jax.shard_map(
        on_device, mesh=mesh, in_specs=in_specs, out_specs=out_specs, check_vma=False
    )
```

```python
import functools

import jax
import jax.numpy as jnp
from jax import lax
from jax.experimental import pallas as pl
from jax.experimental.pallas import tpu as pltpu
from jax.sharding import PartitionSpec as P

SLAB_IMAGES = 4
BLOCK = 512
TILE = 128
EXTRA = 8
PIVOTS = 8
VMEM_LIMIT = 60 * 1024 * 1024

damping = 0.1
point_damping = 0.5

NT = (((1,), (1,)), ((), ()))


def point_terms(pts):
    views = len(pts)
    pairs = [(k, r) for k in range(views) for r in range(2)]

    def entry(left, right):
        return sum(pts[k][r][left] * pts[k][r][right] for k, r in pairs)

    d1 = jnp.sqrt(entry(0, 0) + point_damping)
    b1 = entry(1, 0) / d1
    bf = entry(2, 0) / d1
    d2 = jnp.sqrt(entry(1, 1) + point_damping - b1 * b1)
    b2 = (entry(2, 1) - bf * b1) / d2
    d3 = jnp.sqrt(entry(2, 2) + point_damping - bf * bf - b2 * b2)

    def solve(first, second, third):
        o1 = first / d1
        o2 = (second - b1 * o1) / d2
        o3 = (third - bf * o1 - b2 * o2) / d3
        return [o.astype(jnp.bfloat16).astype(jnp.float32) for o in (o1, o2, o3)]

    coef = {(k, r): solve(*pts[k][r][0:3]) for k, r in pairs}
    step = solve(*[entry(c, 3) for c in range(3)])
    return coef, step


def accumulate_kernel(regions, pos_ref, cam_ref, pts_ref, img_ref, out_ref, acc, rows, cols, dr, dc):
    views = cam_ref.shape[0]
    params = cam_ref.shape[2]
    block = cam_ref.shape[3]
    half = params // 2
    tile_rows = SLAB_IMAGES * half
    step = pl.program_id(0)
    count = pos_ref[lax.axis_index("region")]
    row_at = lax.axis_index("row")
    col_at = lax.axis_index("col")

    @pl.when(step == 0)
    def _():
        acc[...] = jnp.zeros_like(acc)
        rows[tile_rows:, :] = jnp.zeros_like(rows[tile_rows:, :])
        dr[half:, :] = jnp.zeros_like(dr[half:, :])

    @pl.when(step * block < count)
    def _():
        slot = step * block + lax.broadcasted_iota(jnp.int32, (1, block), 1)
        live = slot < count
        pts = []
        for k in range(views):
            pts.append([])
            for r in range(2):
                wide = pts_ref[k, r].astype(jnp.float32)
                pts[k].append([wide[c : c + 1, :] for c in range(4)])
        coef, y = point_terms(pts)
        images = [img_ref[k : k + 1, :] for k in range(views)]

        def picks(image):
            return [(images[k] == image) & live for k in range(views)]

        def pick(masks, values):
            out = jnp.zeros_like(values[0])
            for mask, value in zip(masks, values):
                out = jnp.where(mask, value, out)
            return out

        def chosen(image):
            masks = picks(image)
            c = [
                [pick(masks, [coef[k, r][m] for k in range(views)]) for r in range(2)]
                for m in range(3)
            ]
            return masks, c

        zero = jnp.zeros((15, block), jnp.float32)
        for m in range(3):
            rows[tile_rows : tile_rows + 16, m * block : (m + 1) * block] = jnp.concatenate(
                [y[m], zero], axis=0
            ).astype(jnp.bfloat16)

        sub = 16
        col_masks, col_c = chosen(col_at)
        for r in range(2):
            err = pick(col_masks, [pts[k][r][3] for k in range(views)])
            dr[half : half + 16, r * block : (r + 1) * block] = jnp.concatenate(
                [err, zero], axis=0
            ).astype(jnp.bfloat16)

        def widen(mask):
            return jnp.broadcast_to(mask.astype(jnp.int32), (sub, block)) != 0

        def products(jac, c):
            return [jac[0] * c[m][0] + jac[1] * c[m][1] for m in range(3)]

        def col_chunk(i, _):
            at = pl.multiple_of(i * sub, sub)
            jac = []
            for r in range(2):
                j = [cam_ref[k, r, pl.ds(at, sub), :].astype(jnp.float32) for k in range(views)]
                picked = pick([widen(m) for m in col_masks], j)
                dc[pl.ds(at, sub), r * block : (r + 1) * block] = picked.astype(jnp.bfloat16)
                jac.append(picked)
            for m, value in enumerate(products(jac, col_c)):
                cols[pl.ds(at, sub), m * block : (m + 1) * block] = value.astype(jnp.bfloat16)
            return 0

        lax.fori_loop(0, params // sub, col_chunk, 0)

        row_chosen = [chosen(a) for a in range(SLAB_IMAGES)]

        def row_chunk(i, _):
            at = pl.multiple_of(i * sub, sub)
            src = pl.multiple_of(row_at * half + i * sub, sub)
            j = [
                [cam_ref[k, r, pl.ds(src, sub), :].astype(jnp.float32) for k in range(views)]
                for r in range(2)
            ]
            for a in range(SLAB_IMAGES):
                masks, c = row_chosen[a]
                wide = [widen(m) for m in masks]
                jac = [
                    jnp.where(wide[0], j[r][0], jnp.where(wide[1], j[r][1], j[r][2]))
                    for r in range(2)
                ]
                for m, value in enumerate(products(jac, c)):
                    rows[pl.ds(a * half + at, sub), m * block : (m + 1) * block] = value.astype(
                        jnp.bfloat16
                    )
            return 0

        lax.fori_loop(0, half // sub, row_chunk, 0)
        dr[0:half, :] = dc[pl.ds(pl.multiple_of(row_at * half, half), half), :]
        acc[...] -= lax.dot_general(
            rows[...], cols[...], NT, preferred_element_type=jnp.float32
        )
        direct = lax.dot_general(dr[...], dc[...], NT, preferred_element_type=jnp.float32)
        at = pl.ds(pl.multiple_of(col_at * half, half), half)
        acc[at, :] += direct[0:half]
        acc[tile_rows : tile_rows + 16, :] += direct[half : half + 16]

    @pl.when(step == pl.num_programs(0) - 1)
    def _():
        chunk = tile_rows // regions
        for r in range(regions):
            out_ref[r, 0:chunk, :] = acc[r * chunk : (r + 1) * chunk, :]
            out_ref[r, chunk : chunk + EXTRA, :] = acc[tile_rows : tile_rows + EXTRA, :]


def accumulate(cam_jac, point_rows, track_images, pos, regions):
    views, _, params, slots = cam_jac.shape
    block = min(BLOCK, slots)
    half = params // 2
    tile_rows = SLAB_IMAGES * half
    chunk = tile_rows // regions

    def at(i, pos_ref):
        return jnp.minimum(i, (pos_ref[lax.axis_index("region")] - 1) // block)

    return pl.pallas_call(
        functools.partial(accumulate_kernel, regions),
        out_shape=jax.ShapeDtypeStruct((regions, chunk + EXTRA, params), jnp.float32),
        grid_spec=pltpu.PrefetchScalarGridSpec(
            num_scalar_prefetch=1,
            grid=(slots // block,),
            in_specs=[
                pl.BlockSpec((views, 2, params, block), lambda i, p: (0, 0, 0, at(i, p))),
                pl.BlockSpec((views, 2, 4, block), lambda i, p: (0, 0, 0, at(i, p))),
                pl.BlockSpec((views, block), lambda i, p: (0, at(i, p))),
            ],
            out_specs=pl.BlockSpec((regions, chunk + EXTRA, params), lambda i, p: (0, 0, 0)),
            scratch_shapes=[
                pltpu.VMEM((tile_rows + 16, params), jnp.float32),
                pltpu.VMEM((tile_rows + 16, 3 * block), jnp.bfloat16),
                pltpu.VMEM((params, 3 * block), jnp.bfloat16),
                pltpu.VMEM((half + 16, 2 * block), jnp.bfloat16),
                pltpu.VMEM((params, 2 * block), jnp.bfloat16),
            ],
        ),
        compiler_params=pltpu.CompilerParams(
            dimension_semantics=("arbitrary",), vmem_limit_bytes=VMEM_LIMIT
        ),
        name="accumulate",
    )(pos, cam_jac, point_rows, track_images)


def eliminate(tile):
    groups = TILE // 8
    sub = lax.broadcasted_iota(jnp.int32, (8, TILE), 0)
    lane = lax.broadcasted_iota(jnp.int32, (8, TILE), 1)
    d = [tile[8 * g : 8 * g + 8, :] for g in range(groups)]
    e = [(lane == sub + 8 * g).astype(jnp.float32) for g in range(groups)]
    for j in range(0, TILE, PIVOTS):
        g, s = j // 8, j % 8
        ids = range(PIVOTS)
        rd = [d[g][s + q : s + q + 1, :] for q in ids]
        re = [e[g][s + q : s + q + 1, :] for q in ids]
        block = {
            (p, q): jnp.broadcast_to(rd[p][:, j + q : j + q + 1], (1, TILE))
            for p in ids
            for q in ids
            if q >= p
        }
        low, inv = {}, []
        for p in ids:
            inv.append(1.0 / block[p, p])
            for q in range(p + 1, PIVOTS):
                low[q, p] = block[p, q] * inv[p]
            for q in range(p + 1, PIVOTS):
                for r in range(q, PIVOTS):
                    block[q, r] = block[q, r] - low[q, p] * block[p, r]
                rd[q] = rd[q] - low[q, p] * rd[p]
                re[q] = re[q] - low[q, p] * re[p]
        roots = [lax.rsqrt(block[p, p]) for p in ids]
        wd = [rd[p] * inv[p] for p in ids]
        we = [re[p] * inv[p] for p in ids]
        for q in reversed(ids):
            for p in range(q):
                wd[p] = wd[p] - low[q, p] * wd[q]
                we[p] = we[p] - low[q, p] * we[q]
        wd = [jnp.broadcast_to(w, (8, TILE)) for w in wd]
        we = [jnp.broadcast_to(w, (8, TILE)) for w in we]
        for i in range(g, groups):
            if i == g and s + PIVOTS == 8:
                new_d, new_e = d[i], e[i]
            else:
                new_d, new_e = d[i], e[i]
                for p in ids:
                    col = jnp.broadcast_to(d[i][:, j + p : j + p + 1], (8, TILE))
                    if i == g:
                        col = jnp.where(sub >= s + PIVOTS, col, 0.0)
                    new_d = new_d - col * wd[p]
                    new_e = new_e - col * we[p]
            if i == g:
                for p in ids:
                    new_d = jnp.where(sub == s + p, rd[p] * roots[p], new_d)
                    new_e = jnp.where(sub == s + p, re[p] * roots[p], new_e)
            d[i], e[i] = new_d, new_e
    u = jnp.concatenate([jnp.where(lane >= sub + 8 * g, d[g], 0.0) for g in range(groups)], axis=0)
    return u, jnp.concatenate(e, axis=0)


def factor_kernel(regions, params, all_ref, factor_ref, solved_ref, a_ref, linv_ref):
    total = SLAB_IMAGES * params
    half = params // 2
    chunk = SLAB_IMAGES * half // regions
    for r in range(regions):
        for c in range(2):
            first = (r * chunk) // half * params + c * half + (r * chunk) % half
            for j in range((r * chunk) // half + 1):
                a_ref[first : first + chunk, j * params : (j + 1) * params] = all_ref[
                    (r * 2 + c) * SLAB_IMAGES + j, 0:chunk, :
                ]
    for j in range(SLAB_IMAGES):
        a_ref[total : total + EXTRA, j * params : (j + 1) * params] = all_ref[
            j * half // chunk * 2 * SLAB_IMAGES + j, chunk : chunk + EXTRA, :
        ]
    panels = total // TILE
    eye_r = lax.broadcasted_iota(jnp.int32, (TILE, TILE), 0)
    eye_c = lax.broadcasted_iota(jnp.int32, (TILE, TILE), 1)
    damp = jnp.where(eye_r == eye_c, damping, 0.0).astype(jnp.float32)

    def panel(n, _):
        at = pl.ds(pl.multiple_of(n * TILE, TILE), TILE)
        upper, linv = eliminate(a_ref[at, at] + damp)
        a_ref[at, at] = upper.T
        linv_ref[...] = linv
        for s in range(panels):

            @pl.when(n == s)
            def _():
                lo = s * TILE
                hi = lo + TILE
                below = lax.dot_general(
                    a_ref[hi : total + EXTRA, lo:hi],
                    linv_ref[...],
                    NT,
                    precision=lax.Precision.HIGHEST,
                    preferred_element_type=jnp.float32,
                )
                a_ref[hi : total + EXTRA, lo:hi] = below
                col = hi
                while col < total:
                    width = 2 * TILE if col % (2 * TILE) == 0 else TILE
                    a_ref[col : total + EXTRA, col : col + width] -= lax.dot_general(
                        a_ref[col : total + EXTRA, lo:hi],
                        a_ref[col : col + width, lo:hi],
                        NT,
                        precision=lax.Precision.HIGHEST,
                        preferred_element_type=jnp.float32,
                    )
                    col += width

        return 0

    lax.fori_loop(0, panels, panel, 0)
    row_block = factor_ref.shape[0]
    first_row = pl.multiple_of(
        (lax.axis_index("region") * 2 + lax.axis_index("row")) * row_block, row_block
    )
    first_col = pl.multiple_of(lax.axis_index("col") * params, params)
    held = a_ref[pl.ds(first_row, row_block), pl.ds(first_col, params)]
    at_row = first_row + lax.broadcasted_iota(jnp.int32, held.shape, 0)
    at_col = first_col + lax.broadcasted_iota(jnp.int32, held.shape, 1)
    factor_ref[...] = jnp.where(at_row >= at_col, held, 0.0)
    solved_ref[...] = a_ref[total, :]


def factorize(everything, regions, params, row_block):
    total = SLAB_IMAGES * params
    return pl.pallas_call(
        functools.partial(factor_kernel, regions, params),
        out_shape=(
            jax.ShapeDtypeStruct((row_block, params), jnp.float32),
            jax.ShapeDtypeStruct((total,), jnp.float32),
        ),
        in_specs=[pl.BlockSpec(memory_space=pltpu.VMEM)],
        out_specs=(
            pl.BlockSpec(memory_space=pltpu.VMEM),
            pl.BlockSpec(memory_space=pltpu.VMEM),
        ),
        scratch_shapes=[
            pltpu.VMEM((total + EXTRA, total), jnp.float32),
            pltpu.VMEM((TILE, TILE), jnp.float32),
        ],
        compiler_params=pltpu.CompilerParams(vmem_limit_bytes=VMEM_LIMIT),
        name="factorize",
    )(everything)


def exchange_kernel(regions, tile_ref, all_ref, recv, mine, sum_send, sum_recv, sends, arrived):
    half = recv.shape[2] // 2
    chunk = SLAB_IMAGES * half // regions
    region_at = lax.axis_index("region")
    row_at = lax.axis_index("row")
    col_at = lax.axis_index("col")

    def device(region, row, col):
        return {"region": region, "row": row, "col": col}

    def plus(at, by, size):
        return lax.rem(at + by, size)

    def needed(region, col):
        return (region * chunk) // half >= col

    def index(region, row, col):
        return (region * 2 + row) * SLAB_IMAGES + col

    partner = device(region_at, 1 - row_at, col_at)
    along = [device(plus(region_at, d, regions), row_at, col_at) for d in range(1, regions)]
    side = col_at + 1 - 2 * lax.rem(col_at, 2)
    over = plus(col_at, 2, SLAB_IMAGES)
    corner = SLAB_IMAGES - 1 - col_at
    across = [device(region_at, row_at, side), device(region_at, row_at, over)]
    far = device(region_at, row_at, corner)
    barrier = pltpu.get_barrier_semaphore()
    for peer in [partner, far] + along + across:
        pl.semaphore_signal(barrier, inc=1, device_id=peer, device_id_type=pl.DeviceIdType.MESH)
    pl.semaphore_wait(barrier, regions + SLAB_IMAGES - 1)

    def part(d):
        to = plus(region_at, d, regions)
        return to, pltpu.make_async_remote_copy(
            src_ref=tile_ref.at[to],
            dst_ref=recv.at[d - 1],
            send_sem=sum_send.at[d - 1],
            recv_sem=sum_recv.at[d - 1],
            device_id=device(to, row_at, col_at),
            device_id_type=pl.DeviceIdType.MESH,
        )

    for d in range(1, regions):
        to, copy = part(d)

        @pl.when(needed(to, col_at))
        def _():
            copy.start()

    me = index(region_at, row_at, col_at)

    @pl.when(needed(region_at, col_at))
    def _():
        for d in range(1, regions):
            part(d)[1].wait_recv()
        total = tile_ref[region_at]
        for d in range(1, regions):
            total = total + recv[d - 1]
        mine[...] = total
        all_ref[me] = total

    started = []

    def send(when, src, block, peer):
        copy = pltpu.make_async_remote_copy(
            src_ref=src,
            dst_ref=all_ref.at[block],
            send_sem=sends.at[len(started)],
            recv_sem=arrived.at[block],
            device_id=peer,
            device_id_type=pl.DeviceIdType.MESH,
        )
        started.append((when, copy))

        @pl.when(when)
        def _():
            copy.start()

    def arrive(when, block):
        copy = pltpu.make_async_remote_copy(
            src_ref=all_ref.at[block],
            dst_ref=all_ref.at[block],
            send_sem=sends.at[0],
            recv_sem=arrived.at[block],
            device_id=partner,
            device_id_type=pl.DeviceIdType.MESH,
        )

        @pl.when(when)
        def _():
            copy.wait_recv()

    ok = needed(region_at, col_at)
    for peer in along + across + [partner]:
        send(ok, mine, me, peer)
    for d in range(1, regions):
        origin = plus(region_at, d, regions)
        block = index(origin, row_at, col_at)
        ok = needed(origin, col_at)
        arrive(ok, block)
        for peer in across + [partner]:
            send(ok, all_ref.at[block], block, peer)
    for rd in range(regions):
        origin = plus(region_at, rd, regions)
        for turn, col in enumerate((side, over)):
            block = index(origin, row_at, col)
            ok = needed(origin, col)
            arrive(ok, block)
            onward = jnp.logical_and(ok, lax.rem(origin, 2) == turn)
            send(onward, all_ref.at[block], block, across[1 - turn])
            send(ok, all_ref.at[block], block, partner)
    for rd in range(regions):
        origin = plus(region_at, rd, regions)
        block = index(origin, row_at, corner)
        ok = needed(origin, corner)
        arrive(ok, block)
        send(ok, all_ref.at[block], block, partner)
    for rd in range(regions):
        for cd in range(SLAB_IMAGES):
            origin = plus(region_at, rd, regions)
            col = plus(col_at, cd, SLAB_IMAGES)
            arrive(needed(origin, col), index(origin, 1 - row_at, col))
    for d in range(1, regions):
        to, copy = part(d)

        @pl.when(needed(to, col_at))
        def _():
            copy.wait_send()

    for when, copy in started:

        @pl.when(when)
        def _():
            copy.wait_send()


def exchange(tile):
    regions, depth, params = tile.shape
    blocks = regions * 2 * SLAB_IMAGES
    return pl.pallas_call(
        functools.partial(exchange_kernel, regions),
        out_shape=jax.ShapeDtypeStruct((blocks, depth, params), jnp.float32),
        in_specs=[pl.BlockSpec(memory_space=pltpu.VMEM)],
        out_specs=pl.BlockSpec(memory_space=pltpu.VMEM),
        scratch_shapes=[
            pltpu.VMEM((regions - 1, depth, params), jnp.float32),
            pltpu.VMEM((depth, params), jnp.float32),
            pltpu.SemaphoreType.DMA((regions - 1,)),
            pltpu.SemaphoreType.DMA((regions - 1,)),
            pltpu.SemaphoreType.DMA((blocks + regions,)),
            pltpu.SemaphoreType.DMA((blocks,)),
        ],
        compiler_params=pltpu.CompilerParams(
            collective_id=0, has_side_effects=True, vmem_limit_bytes=VMEM_LIMIT
        ),
        name="exchange",
    )(tile)


def on_device(cam_jac, point_rows, track_images, track_counts):
    regions = lax.axis_size("region")
    row_count = lax.axis_size("row")
    params = cam_jac.shape[2]
    row_block = SLAB_IMAGES * params // (regions * row_count)
    tile = accumulate(cam_jac, point_rows, track_images, track_counts, regions)
    everything = exchange(tile)
    factor, solved = factorize(everything, regions, params, row_block)
    return (factor, solved)


def solution(mesh):
    in_specs = (
        P(None, None, None, "region"),
        P(None, None, None, "region"),
        P(None, "region"),
        P(),
    )
    out_specs = (P(("region", "row"), "col"), P())
    return jax.shard_map(
        on_device, mesh=mesh, in_specs=in_specs, out_specs=out_specs, check_vma=False
    )
```
